1024 devices in a mesh: section: 16 (over y, x_hi, core), fsdp: 32 (over z), tp: 2 (over x_lo).
Axes of the slice: x: 4 (x_hi: 2, x_lo: 2; x = x_hi * 2 + x_lo), y: 4, z: 32, core: 2. Of those that a mesh axis runs over, the one named last changes fastest.
Arguments:
- text_tokens: bfloat16 [65536, 8192], P(('section', 'fsdp')), may hold values from -45 to 45
- images: bfloat16 [256, 256, 8192], P('section', None, ('fsdp', 'tp')), may hold values from -45 to 45
- counts: int32 [256], P('section'), may hold values from 1 to 256, as said below
- offsets: int32 [256], P('section'), may hold values from 0 to 65535, as said below
- norm_gain: float32 [8192], replicated, may hold values from 0.25 to 1.75
- value_weight: bfloat16 [8192, 512], P(('fsdp', 'tp'), 'section'), may hold values from -0.0625 to 0.0625
- value_grad: bfloat16 [65536, 512], P(('section', 'fsdp')), may hold values from -6 to 6
Outputs:
- values: bfloat16 [65536, 512], P(('section', 'fsdp'), 'tp')
- visual_grads: bfloat16 [256, 256, 8192], P('section', None, ('fsdp', 'tp'))
The draws below stay inside these ranges and needn't reach their ends.
Inputs may be any that keep to these rules, and one draw needn't show every extreme that they name: `counts`: on every section index some tile has exactly 256 visual tokens. Tile i occupies positions offsets[i] to offsets[i] + counts[i] - 1, all inside one aligned block of 256 positions. The positions of one section index form 16 such blocks. The 16 tiles of one section index go to 16 different section indices, and every block receives exactly one tile.
All inputs are finite; a program needn't handle non-finite values.
Results may differ from the reference program's by a relative error of at most 0.0049.
Values may be sent and summed in bfloat16 or wider, within the bound.
No kernel may reach another device: no remote copies, remote signals or barrier semaphores. Data moves between devices by JAX's collectives and lax.ppermute only.
A program may use at most 64 MiB of HBM per device.

```python
import math
import jax
import jax.numpy as jnp
from jax import lax

D = 8192
PMAX = 256
IMAGES = 256
TOK_DEV = 128
TOKENS = 65536
VALUE_WIDTH = 512
N_SECTION = 16
N_FSDP = 32


def rough_rows(key, rows, width):
    subkeys = jax.random.split(key, 3)
    row_factor = jnp.exp(jax.random.uniform(subkeys[0], (rows, 1), minval=math.log(0.3), maxval=math.log(3.0)))
    column_factor = jnp.exp(jax.random.uniform(subkeys[1], (1, width), minval=math.log(0.3), maxval=math.log(3.0)))
    base_draw = jnp.clip(jax.random.normal(subkeys[2], (rows, width)), -5.0, 5.0)
    return jnp.clip(base_draw * row_factor * column_factor, -45.0, 45.0)


def draw_text_tokens(key, part):
    return rough_rows(jax.random.fold_in(key, 21), TOKENS, D).astype(jnp.bfloat16)


def draw_images(key, part):
    return rough_rows(jax.random.fold_in(key, 22), IMAGES * PMAX, D).reshape(IMAGES, PMAX, D).astype(jnp.bfloat16)


def placement_draw(key):
    subkeys = jax.random.split(jax.random.fold_in(key, 7), 5)
    sections = N_SECTION
    grid_shape = (sections, sections)
    counts = jax.random.randint(subkeys[0], grid_shape, 1, PMAX + 1)
    full_image = jax.random.randint(subkeys[1], (sections, 1), 0, sections)
    slot_ids = jnp.arange(sections, dtype=jnp.int32)[None, :]
    counts = jnp.where(slot_ids == full_image, PMAX, counts)
    scores = jax.random.randint(subkeys[2], grid_shape, 0, 1 << 20) * sections + slot_ids
    target = jnp.argsort(scores, axis=-1).astype(jnp.int32)
    scores_two = jax.random.randint(subkeys[3], grid_shape, 0, 1 << 20) * sections + slot_ids
    region_perm = jnp.argsort(scores_two, axis=-1).astype(jnp.int32)
    source = jnp.arange(sections, dtype=jnp.int32)[:, None]
    region = region_perm[target, source]
    first_slot = jax.random.randint(subkeys[4], grid_shape, 0, PMAX - counts + 1)
    offsets = target * (N_FSDP * TOK_DEV) + region * PMAX + first_slot
    return (counts.reshape(-1).astype(jnp.int32), offsets.reshape(-1).astype(jnp.int32))


def draw_counts(key, part):
    return placement_draw(key)[0]


def draw_offsets(key, part):
    return placement_draw(key)[1]


def shard_levels(rng, shape, pieces, low, largest):
    gain, own = 1.0, jax.random.fold_in(rng, 6)
    for dim, parts in pieces:
        draws = jnp.exp(jax.random.uniform(jax.random.fold_in(own, dim), (parts,), jnp.float32, low / len(pieces), largest / len(pieces)))
        gain = gain * jnp.repeat(draws, shape[dim] // parts).reshape([-1 if axis == dim else 1 for axis in range(len(shape))])
    return gain


def centred(key, shape, spread, bound, pieces=(), held_as=jnp.bfloat16):
    entries = spread * jax.random.normal(key, shape, jnp.float32)
    if pieces:
        entries = entries * shard_levels(key, shape, pieces, -0.22, 0.18)
    return jnp.clip(entries, -bound, bound).astype(held_as)


def setup_inputs(seed: int = 0) -> dict:
    keys = jax.random.split(jax.random.key(seed), 8)
    return {
        "text_tokens": draw_text_tokens(jax.random.fold_in(keys[7], 71), 0),
        "images": draw_images(jax.random.fold_in(keys[7], 71), 0),
        "counts": draw_counts(jax.random.fold_in(keys[7], 71), 0),
        "offsets": draw_offsets(jax.random.fold_in(keys[7], 71), 0),
        "norm_gain": jnp.clip(1.0 + 0.15 * jax.random.normal(keys[4], (D,), jnp.float32), 0.25, 1.75),
        "value_weight": centred(keys[5], (D, VALUE_WIDTH), D ** -0.5, 0.0625, ((0, 64), (1, 16))),
        "value_grad": centred(keys[6], (TOKENS, VALUE_WIDTH), 1.0, 6.0, ((0, 512),)),
    }


epsilon = 1e-05

def row_scale(rows):
    values_f = rows.astype(jnp.float32)
    return lax.rsqrt(lax.optimization_barrier(jnp.mean(values_f * values_f, axis=-1, keepdims=True)) + epsilon)

def normalize(rows, norm_gain):
    inv_rms = row_scale(rows)
    return (rows.astype(jnp.float32) * inv_rms * norm_gain).astype(jnp.bfloat16)

def norm_back(rows, inv_rms, norm_gain, grad_normed):
    values_f = rows.astype(jnp.float32)
    weighted = grad_normed * norm_gain
    inner_dot = lax.optimization_barrier(jnp.sum(weighted * values_f, axis=-1, keepdims=True))
    return inv_rms * weighted - values_f * (inv_rms * inv_rms * inv_rms) * inner_dot / rows.shape[-1]

def reference(text_tokens, images, counts, offsets, norm_gain, value_weight, value_grad):
    slot_idx = jnp.arange(PMAX, dtype=jnp.int32)
    is_valid = slot_idx[None, :] < counts[:, None]
    position = jnp.where(is_valid, offsets[:, None] + slot_idx[None, :], TOKENS).reshape(-1).astype(jnp.int32)
    flat_images = images.reshape(-1, D)
    mixed_rows = text_tokens.at[position].set(flat_images, mode='drop')

    def project(row_block):
        normed = normalize(row_block, norm_gain)
        return jnp.dot(normed, value_weight, preferred_element_type=jnp.float32).astype(jnp.bfloat16)
    values = lax.map(project, mixed_rows.reshape(-1, TOK_DEV, D)).reshape(TOKENS, VALUE_WIDTH)
    valid_flat = is_valid.reshape(-1)
    safe_pos = jnp.where(valid_flat, position, 0).astype(jnp.int32)
    slot_grad = jnp.where(valid_flat[:, None], value_grad[safe_pos], jnp.zeros((), jnp.bfloat16))

    def backward(pair):
        rows, grad_rows = pair
        grad_normed = jnp.dot(grad_rows, value_weight.T, preferred_element_type=jnp.float32)
        return norm_back(rows, row_scale(rows), norm_gain, grad_normed).astype(jnp.bfloat16)
    visual_grads = lax.map(backward, (images, slot_grad.reshape(IMAGES, PMAX, VALUE_WIDTH)))
    return (values, visual_grads)
```

```python
import jax
import jax.numpy as jnp
from jax import lax
from jax.sharding import PartitionSpec as P


epsilon = 1e-05


def swapped(x, axis, bit):
    length = lax.axis_size(axis)
    return lax.ppermute(x, axis, [(i, i ^ bit) for i in range(length)])


def joined(x, axis, bit):
    other = swapped(x, axis, bit)
    is_high = (lax.axis_index(axis) & bit) != 0
    return jnp.stack([jnp.where(is_high, other, x), jnp.where(is_high, x, other)])


def gathered_by_bits(x, axis):
    length = lax.axis_size(axis)
    rest = x.shape
    bits = length.bit_length() - 1
    for b in range(bits - 1, -1, -1):
        x = joined(x, axis, 1 << b)
    order = tuple(range(bits - 1, -1, -1))
    return x.transpose(order + tuple(range(bits, bits + len(rest)))).reshape(length, *rest)


def on_device(text_tokens, images, counts, offsets, norm_gain, value_weight, value_grad):
    sections = lax.axis_size("section")
    columns = lax.axis_size("fsdp")
    pair_count = lax.axis_size("tp")
    tok_rows, feature_width = text_tokens.shape
    img_count, most_slots, feature_slice = images.shape
    width = value_grad.shape[1]
    half_width = width // pair_count
    half_rows = tok_rows // pair_count
    halves = most_slots // tok_rows
    group_rows = columns * tok_rows
    pair_index = lax.axis_index("tp")
    column_index = lax.axis_index("fsdp")
    plane = ("section", "tp")

    own_half = lax.dynamic_index_in_dim(
        value_grad.reshape(pair_count, half_rows, width), pair_index, 0, keepdims=False
    )
    grads_in = lax.all_gather(own_half, "fsdp", axis=0, tiled=True)

    target = offsets // group_rows
    within = offsets % group_rows
    region = within // most_slots
    first_slot = within % most_slots
    section_ids = jnp.arange(sections, dtype=jnp.int32)
    slot_ids = jnp.arange(most_slots, dtype=jnp.int32)
    is_valid = slot_ids[None, :] < counts[:, None]
    placing = (
        (slot_ids[None, :, None] == first_slot[:, None, None] + slot_ids[None, None, :])
        & is_valid[:, None, :]
    ).astype(jnp.bfloat16)
    routing = target[:, None] == section_ids[None, :]
    route_float = routing.astype(jnp.bfloat16)
    route_int = routing.astype(jnp.int32)
    meta_rows = jnp.stack([region, first_slot, counts], axis=1)
    meta_out = jnp.sum(route_int[:, :, None] * meta_rows[:, None, :], axis=0)
    meta_in = lax.all_to_all(meta_out, "section", split_axis=0, concat_axis=0, tiled=True)

    placed = jnp.einsum("krj,kjd->krd", placing, images, preferred_element_type=jnp.float32).astype(
        jnp.bfloat16
    )
    outgoing = jnp.einsum(
        "kt,krd->trd", route_float, placed, preferred_element_type=jnp.float32
    ).astype(jnp.bfloat16)
    arrived = lax.all_to_all(outgoing, "section", split_axis=0, concat_axis=0, tiled=True)
    order_int = (meta_in[:, 0:1] == section_ids[None, :]).astype(jnp.int32)
    order_float = order_int.astype(jnp.bfloat16)
    by_region = jnp.einsum(
        "sr,spd->rpd", order_float, arrived, preferred_element_type=jnp.float32
    ).astype(jnp.bfloat16)
    rows_in = lax.all_to_all(
        by_region.reshape(columns, tok_rows, feature_slice),
        "fsdp",
        split_axis=0,
        concat_axis=0,
        tiled=True,
    )

    w_start, text_tokens, _ = lax.optimization_barrier((value_weight.T, text_tokens, by_region))
    w_rows = gathered_by_bits(w_start, "fsdp")
    w_all = gathered_by_bits(w_rows.transpose(1, 0, 2), "section")
    w_all = w_all.reshape(width, columns, feature_slice)
    gain_pairs = norm_gain.reshape(columns, pair_count, feature_slice)
    gain_own = lax.dynamic_index_in_dim(gain_pairs, pair_index, 1, keepdims=False)
    w_gain = (w_all.astype(jnp.float32) * gain_own[None]).astype(jnp.bfloat16)
    w_here = lax.dynamic_index_in_dim(w_all, column_index, 1, keepdims=False)
    w_pair = joined(w_here, "tp", 1)
    gain_here = lax.dynamic_index_in_dim(gain_pairs, column_index, 0, keepdims=False)

    region_start = jnp.sum(order_int * meta_in[:, 1:2], axis=0)
    region_count = jnp.sum(order_int * meta_in[:, 2:3], axis=0)
    row_ids = column_index * tok_rows + jnp.arange(tok_rows, dtype=jnp.int32)
    row_region = ((row_ids // most_slots)[:, None] == section_ids[None, :]).astype(jnp.int32)
    row_local = row_ids % most_slots
    row_start = jnp.sum(row_region * region_start[None, :], axis=1)
    row_count = jnp.sum(row_region * region_count[None, :], axis=1)
    covered = (row_local >= row_start) & (row_local < row_start + row_count)

    text_own = lax.dynamic_index_in_dim(
        text_tokens.reshape(tok_rows, columns, pair_count, feature_slice),
        pair_index,
        2,
        keepdims=False,
    )
    text_f = text_own.astype(jnp.float32)
    text_square = jnp.sum(text_f * text_f, axis=(1, 2))
    text_raw = lax.dot_general(
        text_own.reshape(tok_rows, -1),
        w_gain.reshape(width, -1),
        (((1,), (1,)), ((), ())),
        preferred_element_type=jnp.float32,
    )

    rows_f = rows_in.astype(jnp.float32)
    row_square = jnp.sum(rows_f * rows_f, axis=(0, 2))
    row_raw = lax.dot_general(
        rows_in.transpose(1, 0, 2).reshape(tok_rows, -1),
        w_gain.reshape(width, -1),
        (((1,), (1,)), ((), ())),
        preferred_element_type=jnp.float32,
    )
    row_inner = jnp.sum(row_raw * value_grad.astype(jnp.float32), axis=1)

    sums = jnp.stack([row_square, row_inner])
    sums_in = lax.all_to_all(
        jnp.broadcast_to(sums[None], (columns, *sums.shape)), "fsdp", 0, 0, tiled=True
    )
    sums_region = sums_in.reshape(sections, -1)
    order_f32 = order_int.astype(jnp.float32)
    sums_source = jnp.sum(order_f32[:, :, None] * sums_region[None], axis=1)
    sums_both = jnp.broadcast_to(
        sums_source[:, None], (sections, pair_count, sums_source.shape[1])
    ).reshape(sections * pair_count, 8, -1)
    sums_back = lax.all_to_all(sums_both, plane, 0, 0, tiled=True)
    sums_back = jnp.sum(sums_back.reshape(sections, pair_count, -1), axis=1)
    sums_tile = jnp.sum(
        routing.astype(jnp.float32)[:, :, None] * sums_back[None], axis=1
    ).reshape(img_count, halves, 2, tok_rows)
    tile_square = sums_tile[:, :, 0].reshape(img_count, most_slots)
    tile_inner = sums_tile[:, :, 1].reshape(img_count, most_slots)

    raw = jnp.where(covered[:, None], row_raw, text_raw)
    square = jnp.where(covered, row_square, text_square)
    low, high = raw[:, :half_width], raw[:, half_width:]
    is_second = pair_index == 1
    kept = jnp.where(is_second, high, low)
    sent = jnp.where(is_second, low, high)
    lanes = jnp.broadcast_to(square[:, None], (tok_rows, 128))
    got = swapped(jnp.concatenate([sent, lanes], axis=1), "tp", 1)
    full_square = square + got[:, half_width]
    inv_rms = lax.rsqrt(full_square / feature_width + epsilon)[:, None]
    values = ((kept + got[:, :half_width]) * inv_rms).astype(jnp.bfloat16)

    w_pair, _ = lax.optimization_barrier((w_pair, rows_in))
    weighted = jnp.einsum("rn,tnd->rtd", grads_in, w_pair, preferred_element_type=jnp.float32)
    weighted = (weighted * gain_here[None]).astype(jnp.bfloat16)
    weighted = weighted.reshape(sections, halves * half_rows, pair_count, feature_slice)
    by_source = jnp.einsum(
        "sr,rptd->stpd", order_float, weighted, preferred_element_type=jnp.float32
    ).astype(jnp.bfloat16)
    returned = lax.all_to_all(
        by_source.reshape(sections * pair_count, halves * half_rows, feature_slice),
        plane,
        split_axis=0,
        concat_axis=0,
        tiled=True,
    )
    returned = returned.reshape(sections, pair_count, halves, half_rows, feature_slice)
    returned = returned.transpose(0, 2, 1, 3, 4).reshape(sections, most_slots, feature_slice)
    own_weighted = jnp.einsum(
        "kt,trd->krd", route_float, returned, preferred_element_type=jnp.float32
    )
    tile_inv = lax.rsqrt(tile_square / feature_width + epsilon)
    tile_factor = tile_inv * tile_inv * tile_inv * tile_inner / feature_width
    grad_rows = (
        tile_inv[:, :, None] * own_weighted
        - placed.astype(jnp.float32) * tile_factor[:, :, None]
    ).astype(jnp.bfloat16)
    visual_grads = jnp.einsum(
        "krj,krd->kjd", placing, grad_rows, preferred_element_type=jnp.float32
    ).astype(jnp.bfloat16)
    return (values, visual_grads)


def solution(mesh):
    placed = (
        P(("section", "fsdp"), None),
        P("section", None, ("fsdp", "tp")),
        P("section"),
        P("section"),
        P(),
        P(("fsdp", "tp"), "section"),
        P(("section", "fsdp"), None),
    )

    return jax.shard_map(
        on_device,
        mesh=mesh,
        in_specs=placed,
        out_specs=(P(("section", "fsdp"), "tp"), P("section", None, ("fsdp", "tp"))),
        check_vma=False,
    )
```

```python
import jax
import jax.numpy as jnp
from jax import lax
from jax.sharding import PartitionSpec as P


epsilon = 1e-05


def swapped(x, axis, bit):
    length = lax.axis_size(axis)
    return lax.ppermute(x, axis, [(i, i ^ bit) for i in range(length)])


def joined(x, axis, bit):
    other = swapped(x, axis, bit)
    is_high = (lax.axis_index(axis) & bit) != 0
    return jnp.stack([jnp.where(is_high, other, x), jnp.where(is_high, x, other)])


def gathered_by_bits(x, axis):
    length = lax.axis_size(axis)
    rest = x.shape
    bits = length.bit_length() - 1
    for b in range(bits - 1, -1, -1):
        x = joined(x, axis, 1 << b)
    order = tuple(range(bits - 1, -1, -1))
    return x.transpose(order + tuple(range(bits, bits + len(rest)))).reshape(length, *rest)


def fetched(x, axis, distance):
    length = lax.axis_size(axis)
    return lax.ppermute(x, axis, [(i, (i - distance) % length) for i in range(length)])


def gathered_by_windows(x, axis):
    length = lax.axis_size(axis)
    strides = length // 8
    far = [x]
    for a in range(1, strides):
        far.append(fetched(x, axis, 8 * a))
    far = jnp.stack(far)
    ahead, ahead2, behind = (fetched(far, axis, d) for d in (2, 4, -2))
    behind = jnp.concatenate([behind[1:], behind[:1]])
    even = jnp.stack([behind, far, ahead, ahead2])
    above = fetched(even[1:3], axis, 1)
    below = fetched(even[0:2], axis, -1)
    last = jnp.concatenate([below[1, 1:], below[1, :1]])
    pieces = [far, above[0], ahead, above[1], ahead2, below[0], behind, last]
    relative = jnp.stack(pieces, axis=1).reshape(length, *x.shape)
    twice = jnp.concatenate([relative, relative])
    return lax.dynamic_slice_in_dim(twice, length - lax.axis_index(axis), length, 0)


def on_device(text_tokens, images, counts, offsets, norm_gain, value_weight, value_grad):
    sections = lax.axis_size("section")
    columns = lax.axis_size("fsdp")
    pair_count = lax.axis_size("tp")
    tok_rows, feature_width = text_tokens.shape
    img_count, most_slots, feature_slice = images.shape
    width = value_grad.shape[1]
    own_columns = value_weight.shape[1]
    half_width = width // pair_count
    half_rows = tok_rows // pair_count
    halves = most_slots // tok_rows
    group_rows = columns * tok_rows
    pair_index = lax.axis_index("tp")
    column_index = lax.axis_index("fsdp")
    is_second = pair_index == 1
    plane = ("section", "tp")
    w_rows_first = value_weight.T

    own_half = lax.dynamic_index_in_dim(
        value_grad.reshape(pair_count, half_rows, width), pair_index, 0, keepdims=False
    )
    own_half = lax.optimization_barrier(own_half)
    sent_rows = jnp.concatenate([own_half, w_rows_first.reshape(-1, width)])
    column_rows = gathered_by_windows(sent_rows, "fsdp")
    grads_in = column_rows[:, :half_rows]
    w_column = column_rows[:, half_rows:].reshape(columns, own_columns, feature_slice)

    target = offsets // group_rows
    within = offsets % group_rows
    region = within // most_slots
    first_slot = within % most_slots
    section_ids = jnp.arange(sections, dtype=jnp.int32)
    slot_ids = jnp.arange(most_slots, dtype=jnp.int32)
    is_valid = slot_ids[None, :] < counts[:, None]
    placing = (
        (slot_ids[None, :, None] == first_slot[:, None, None] + slot_ids[None, None, :])
        & is_valid[:, None, :]
    ).astype(jnp.bfloat16)
    routing = target[:, None] == section_ids[None, :]
    route_float = routing.astype(jnp.bfloat16)
    route_int = routing.astype(jnp.int32)
    meta_rows = jnp.stack([region, first_slot, counts], axis=1)
    meta_out = jnp.sum(route_int[:, :, None] * meta_rows[:, None, :], axis=0)
    meta_in = lax.all_to_all(meta_out, "section", split_axis=0, concat_axis=0, tiled=True)

    placed = jnp.einsum("krj,kjd->krd", placing, images, preferred_element_type=jnp.float32).astype(
        jnp.bfloat16
    )
    outgoing = jnp.einsum(
        "kt,krd->trd", route_float, placed, preferred_element_type=jnp.float32
    ).astype(jnp.bfloat16)
    outgoing = outgoing.reshape(sections, halves, pair_count, half_rows, feature_slice)
    outgoing = outgoing.transpose(0, 2, 1, 3, 4).reshape(-1, halves * half_rows, feature_slice)
    w_copies = jnp.broadcast_to(w_rows_first[None], (outgoing.shape[0], *w_rows_first.shape))
    arrived = lax.all_to_all(jnp.concatenate([outgoing, w_copies], axis=1), plane, 0, 0, tiled=True)
    arrived = arrived.reshape(sections, pair_count, -1, feature_slice)
    w_here = arrived[:, :, halves * half_rows :]
    order_int = (meta_in[:, 0:1] == section_ids[None, :]).astype(jnp.int32)
    order_float = order_int.astype(jnp.bfloat16)
    rows = jnp.einsum(
        "sr,stpd->trpd",
        order_float,
        arrived[:, :, : halves * half_rows],
        preferred_element_type=jnp.float32,
    ).astype(jnp.bfloat16)
    rows = rows.reshape(pair_count, columns * half_rows, feature_slice)
    w_here = w_here.transpose(1, 0, 2, 3).reshape(pair_count, width, feature_slice)
    gain_pairs = norm_gain.reshape(columns, pair_count, feature_slice)
    gain_here = lax.dynamic_index_in_dim(gain_pairs, column_index, 0, keepdims=False)
    w_here_gain = (w_here.astype(jnp.float32) * gain_here[:, None, :]).astype(jnp.bfloat16)

    part = sum(
        lax.dot_general(
            rows[t],
            w_here_gain[t],
            (((1,), (1,)), ((), ())),
            preferred_element_type=jnp.float32,
        )
        for t in range(pair_count)
    )
    rows_f = [rows[t].astype(jnp.float32) for t in range(pair_count)]
    squares = jnp.sum(sum(r * r for r in rows_f), axis=1, keepdims=True)
    part = jnp.concatenate([part, jnp.broadcast_to(squares, (squares.shape[0], 128))], axis=1)
    own_sums = lax.psum_scatter(part, "fsdp", scatter_dimension=0, tiled=True)
    image_raw = own_sums[:, :width]
    own_inv = lax.rsqrt(own_sums[:, width] / feature_width + epsilon)
    own_inner = jnp.sum(image_raw * own_half.astype(jnp.float32), axis=1)
    own_factor = own_inv * own_inv * own_inv * own_inner / feature_width

    scalars = jnp.stack([own_inv, own_factor]).reshape(1, 1, -1)
    scalars = lax.all_to_all(
        jnp.broadcast_to(scalars, (columns, 1, 2 * half_rows)), "fsdp", 0, 0, tiled=True
    )
    scalars = scalars.reshape(sections, -1)
    scalars = jnp.sum(order_int.astype(jnp.float32)[:, :, None] * scalars[None], axis=1)
    scalars = jnp.broadcast_to(scalars[:, None], (sections, pair_count, scalars.shape[1]))
    scalars = lax.all_to_all(scalars.reshape(sections * pair_count, 2, -1), plane, 0, 0, tiled=True)
    scalars = scalars.reshape(1, sections, -1)
    scalars = jnp.sum(routing.astype(jnp.float32)[:, :, None] * scalars, axis=1)
    scalars = scalars.reshape(img_count, pair_count, halves, 2, half_rows).transpose(0, 3, 2, 1, 4)
    scalars = scalars.reshape(img_count, 2, most_slots)

    grads_flat = grads_in.reshape(-1, width)
    by_source = []
    for t in range(pair_count):
        weighted = lax.dot_general(
            grads_flat, w_here[t], (((1,), (0,)), ((), ())), preferred_element_type=jnp.float32
        )
        weighted = (weighted * gain_here[t]).astype(jnp.bfloat16)
        weighted = weighted.reshape(sections, halves * half_rows, feature_slice)
        by_source.append(
            jnp.einsum("sr,rpd->spd", order_float, weighted, preferred_element_type=jnp.float32)
        )
    by_source = jnp.stack(by_source, axis=1).astype(jnp.bfloat16)
    returned = lax.all_to_all(
        by_source.reshape(-1, halves * half_rows, feature_slice), plane, 0, 0, tiled=True
    )
    returned = returned.reshape(sections, pair_count, halves, half_rows, feature_slice)
    returned = returned.transpose(0, 2, 1, 3, 4).reshape(sections, most_slots, feature_slice)
    own_weighted = jnp.einsum(
        "kt,trd->krd", route_float, returned, preferred_element_type=jnp.float32
    )
    grad_rows = (
        scalars[:, 0, :, None] * own_weighted
        - placed.astype(jnp.float32) * scalars[:, 1, :, None]
    ).astype(jnp.bfloat16)
    visual_grads = jnp.einsum(
        "krj,krd->kjd", placing, grad_rows, preferred_element_type=jnp.float32
    ).astype(jnp.bfloat16)

    w_all = gathered_by_bits(w_column.transpose(1, 0, 2), "section").reshape(width, -1)
    text_split = text_tokens.reshape(tok_rows, columns, pair_count, feature_slice)
    text_own = lax.dynamic_index_in_dim(text_split, pair_index, 2, keepdims=False)
    gain_own = lax.dynamic_index_in_dim(gain_pairs, pair_index, 1, keepdims=False)
    text_gain = (text_own.astype(jnp.float32) * gain_own[None]).astype(jnp.bfloat16)
    text_f = text_tokens.astype(jnp.float32)
    text_inv = lax.rsqrt(jnp.sum(text_f * text_f, axis=1, keepdims=True) / feature_width + epsilon)
    text_raw = lax.dot_general(
        text_gain.reshape(tok_rows, -1),
        w_all,
        (((1,), (1,)), ((), ())),
        preferred_element_type=jnp.float32,
    )
    text_kept = jnp.where(is_second, text_raw[:, half_width:], text_raw[:, :half_width])
    text_sent = jnp.where(is_second, text_raw[:, :half_width], text_raw[:, half_width:])
    text_got = swapped(text_sent, "tp", 1)
    text_values = ((text_kept + text_got) * text_inv).astype(jnp.bfloat16)

    image_values = (image_raw * own_inv[:, None]).astype(jnp.bfloat16)
    image_kept = jnp.where(is_second, image_values[:, half_width:], image_values[:, :half_width])
    image_sent = jnp.where(is_second, image_values[:, :half_width], image_values[:, half_width:])
    image_got = swapped(image_sent, "tp", 1)
    image_rows = jnp.concatenate(
        [
            jnp.where(is_second, image_got, image_kept),
            jnp.where(is_second, image_kept, image_got),
        ]
    )

    region_start = jnp.sum(order_int * meta_in[:, 1:2], axis=0)
    region_count = jnp.sum(order_int * meta_in[:, 2:3], axis=0)
    row_ids = column_index * tok_rows + jnp.arange(tok_rows, dtype=jnp.int32)
    row_region = ((row_ids // most_slots)[:, None] == section_ids[None, :]).astype(jnp.int32)
    row_local = row_ids % most_slots
    row_start = jnp.sum(row_region * region_start[None, :], axis=1)
    row_count = jnp.sum(row_region * region_count[None, :], axis=1)
    covered = (row_local >= row_start) & (row_local < row_start + row_count)
    values = jnp.where(covered[:, None], image_rows, text_values)
    return (values, visual_grads)


def solution(mesh):
    placed = (
        P(("section", "fsdp"), None),
        P("section", None, ("fsdp", "tp")),
        P("section"),
        P("section"),
        P(),
        P(("fsdp", "tp"), "section"),
        P(("section", "fsdp"), None),
    )

    return jax.shard_map(
        on_device,
        mesh=mesh,
        in_specs=placed,
        out_specs=(P(("section", "fsdp"), "tp"), P("section", None, ("fsdp", "tp"))),
        check_vma=False,
    )
```

```python
import jax
import jax.numpy as jnp
from jax import lax
from jax.sharding import PartitionSpec as P


epsilon = 1e-05


def swapped(x, axis, bit):
    length = lax.axis_size(axis)
    return lax.ppermute(x, axis, [(i, i ^ bit) for i in range(length)])


def joined(x, axis, bit):
    other = swapped(x, axis, bit)
    is_high = (lax.axis_index(axis) & bit) != 0
    return jnp.stack([jnp.where(is_high, other, x), jnp.where(is_high, x, other)])


def gathered_by_bits(x, axis):
    length = lax.axis_size(axis)
    rest = x.shape
    bits = length.bit_length() - 1
    for b in range(bits - 1, -1, -1):
        x = joined(x, axis, 1 << b)
    order = tuple(range(bits - 1, -1, -1))
    return x.transpose(order + tuple(range(bits, bits + len(rest)))).reshape(length, *rest)


def fetched(x, axis, distance):
    length = lax.axis_size(axis)
    return lax.ppermute(x, axis, [(i, (i - distance) % length) for i in range(length)])


def gathered_by_windows(x, axis):
    length = lax.axis_size(axis)
    strides = length // 8
    far = [x]
    for a in range(1, strides):
        far.append(fetched(x, axis, 8 * a))
    far = jnp.stack(far)
    ahead, ahead2, behind = (fetched(far, axis, d) for d in (2, 4, -2))
    behind = jnp.concatenate([behind[1:], behind[:1]])
    even = jnp.stack([behind, far, ahead, ahead2])
    above = fetched(even[1:3], axis, 1)
    below = fetched(even[0:2], axis, -1)
    last = jnp.concatenate([below[1, 1:], below[1, :1]])
    pieces = [far, above[0], ahead, above[1], ahead2, below[0], behind, last]
    relative = jnp.stack(pieces, axis=1).reshape(length, *x.shape)
    twice = jnp.concatenate([relative, relative])
    return lax.dynamic_slice_in_dim(twice, length - lax.axis_index(axis), length, 0)


def on_device(text_tokens, images, counts, offsets, norm_gain, value_weight, value_grad):
    sections = lax.axis_size("section")
    columns = lax.axis_size("fsdp")
    pair_count = lax.axis_size("tp")
    tok_rows, feature_width = text_tokens.shape
    _, most_slots, feature_slice = images.shape
    width = value_grad.shape[1]
    own_columns = value_weight.shape[1]
    half_width = width // pair_count
    half_rows = tok_rows // pair_count
    halves = most_slots // tok_rows
    group_rows = columns * tok_rows
    pair_index = lax.axis_index("tp")
    column_index = lax.axis_index("fsdp")
    is_second = pair_index == 1
    plane = ("section", "tp")
    w_rows_first = value_weight.T

    own_half = lax.dynamic_index_in_dim(
        value_grad.reshape(pair_count, half_rows, width), pair_index, 0, keepdims=False
    )
    sent_rows = jnp.concatenate([own_half, w_rows_first.reshape(-1, width)])
    column_rows = gathered_by_windows(sent_rows, "fsdp")
    grads_in = column_rows[:, :half_rows]
    w_column = column_rows[:, half_rows:].reshape(columns, own_columns, feature_slice)

    target = offsets // group_rows
    within = offsets % group_rows
    region = within // most_slots
    first_slot = within % most_slots
    section_ids = jnp.arange(sections, dtype=jnp.int32)
    slot_ids = jnp.arange(most_slots, dtype=jnp.int32)
    is_valid = slot_ids[None, :] < counts[:, None]
    placing = (
        (slot_ids[None, :, None] == first_slot[:, None, None] + slot_ids[None, None, :])
        & is_valid[:, None, :]
    ).astype(jnp.bfloat16)
    routing = target[:, None] == section_ids[None, :]
    route_float = routing.astype(jnp.bfloat16)
    route_int = routing.astype(jnp.int32)
    meta_rows = jnp.stack([region, first_slot, counts], axis=1)
    meta_out = jnp.sum(route_int[:, :, None] * meta_rows[:, None, :], axis=0)
    meta_in = lax.all_to_all(meta_out, "section", split_axis=0, concat_axis=0, tiled=True)

    placed = jnp.einsum("krj,kjd->krd", placing, images, preferred_element_type=jnp.float32).astype(
        jnp.bfloat16
    )
    outgoing = jnp.einsum(
        "kt,krd->trd", route_float, placed, preferred_element_type=jnp.float32
    ).astype(jnp.bfloat16)
    outgoing = outgoing.reshape(sections, halves, pair_count, half_rows, feature_slice)
    outgoing = outgoing.transpose(0, 2, 1, 3, 4).reshape(-1, halves * half_rows, feature_slice)
    w_copies = jnp.broadcast_to(w_rows_first[None], (outgoing.shape[0], *w_rows_first.shape))
    arrived = lax.all_to_all(jnp.concatenate([outgoing, w_copies], axis=1), plane, 0, 0, tiled=True)
    arrived = arrived.reshape(sections, pair_count, -1, feature_slice)
    w_here = arrived[:, :, halves * half_rows :]
    order_int = (meta_in[:, 0:1] == section_ids[None, :]).astype(jnp.int32)
    order_float = order_int.astype(jnp.bfloat16)
    rows = jnp.einsum(
        "sr,stpd->trpd",
        order_float,
        arrived[:, :, : halves * half_rows],
        preferred_element_type=jnp.float32,
    ).astype(jnp.bfloat16)
    rows = rows.reshape(pair_count, columns * half_rows, feature_slice)
    w_here = w_here.transpose(1, 0, 2, 3).reshape(pair_count, width, feature_slice)
    gain_pairs = norm_gain.reshape(columns, pair_count, feature_slice)
    gain_here = lax.dynamic_index_in_dim(gain_pairs, column_index, 0, keepdims=False)
    w_here_gain = (w_here.astype(jnp.float32) * gain_here[:, None, :]).astype(jnp.bfloat16)

    part = sum(
        lax.dot_general(
            rows[t],
            w_here_gain[t],
            (((1,), (1,)), ((), ())),
            preferred_element_type=jnp.float32,
        )
        for t in range(pair_count)
    )
    image_raw = lax.psum_scatter(part, "fsdp", scatter_dimension=0, tiled=True)

    grads_flat = grads_in.reshape(-1, width)
    weighted = [
        lax.dot_general(
            grads_flat,
            w_here[t],
            (((1,), (0,)), ((), ())),
            preferred_element_type=jnp.float32,
        )
        * gain_here[t]
        for t in range(pair_count)
    ]
    rows_f = [rows[t].astype(jnp.float32) for t in range(pair_count)]
    sums = jnp.stack(
        [
            jnp.sum(sum(r * r for r in rows_f), axis=1),
            jnp.sum(sum(w * r for w, r in zip(weighted, rows_f)), axis=1),
        ]
    )
    sums = sums.reshape(2, columns, half_rows).transpose(1, 0, 2).reshape(columns, 1, -1)
    sums_own = lax.all_to_all(sums, "fsdp", 0, 0, tiled=True)
    sums_own = jnp.sum(sums_own, axis=0, keepdims=True)
    sums_all = lax.all_to_all(
        jnp.broadcast_to(sums_own, sums.shape), "fsdp", 0, 0, tiled=True
    )
    sums_all = sums_all.reshape(columns, 2, half_rows)
    row_inv = lax.rsqrt(sums_all[:, 0].reshape(-1) / feature_width + epsilon)
    row_factor = row_inv * row_inv * row_inv * sums_all[:, 1].reshape(-1) / feature_width
    by_source = []
    for t in range(pair_count):
        grad_rows = (
            row_inv[:, None] * weighted[t] - rows_f[t] * row_factor[:, None]
        ).astype(jnp.bfloat16)
        grad_rows = grad_rows.reshape(sections, halves * half_rows, feature_slice)
        by_source.append(
            jnp.einsum("sr,rpd->spd", order_float, grad_rows, preferred_element_type=jnp.float32)
        )
    by_source = jnp.stack(by_source, axis=1).astype(jnp.bfloat16)
    returned = lax.all_to_all(
        by_source.reshape(-1, halves * half_rows, feature_slice), plane, 0, 0, tiled=True
    )
    returned = returned.reshape(sections, pair_count, halves, half_rows, feature_slice)
    returned = returned.transpose(0, 2, 1, 3, 4).reshape(sections, most_slots, feature_slice)
    own_rows = jnp.einsum(
        "kt,trd->krd", route_float, returned, preferred_element_type=jnp.float32
    ).astype(jnp.bfloat16)
    visual_grads = jnp.einsum(
        "krj,krd->kjd", placing, own_rows, preferred_element_type=jnp.float32
    ).astype(jnp.bfloat16)

    w_all = gathered_by_bits(w_column.transpose(1, 0, 2), "section").reshape(width, -1)
    text_split = text_tokens.reshape(tok_rows, columns, pair_count, feature_slice)
    text_own = lax.dynamic_index_in_dim(text_split, pair_index, 2, keepdims=False)
    gain_own = lax.dynamic_index_in_dim(gain_pairs, pair_index, 1, keepdims=False)
    text_gain = (text_own.astype(jnp.float32) * gain_own[None]).astype(jnp.bfloat16)
    text_f = text_tokens.astype(jnp.float32)
    text_inv = lax.rsqrt(jnp.sum(text_f * text_f, axis=1, keepdims=True) / feature_width + epsilon)
    text_raw = lax.dot_general(
        text_gain.reshape(tok_rows, -1),
        w_all,
        (((1,), (1,)), ((), ())),
        preferred_element_type=jnp.float32,
    )
    text_kept = jnp.where(is_second, text_raw[:, half_width:], text_raw[:, :half_width])
    text_sent = jnp.where(is_second, text_raw[:, :half_width], text_raw[:, half_width:])
    text_got = swapped(text_sent, "tp", 1)
    text_values = ((text_kept + text_got) * text_inv).astype(jnp.bfloat16)

    own_inv = lax.rsqrt(sums_own.reshape(2, half_rows)[0] / feature_width + epsilon)
    image_values = (image_raw * own_inv[:, None]).astype(jnp.bfloat16)
    image_kept = jnp.where(is_second, image_values[:, half_width:], image_values[:, :half_width])
    image_sent = jnp.where(is_second, image_values[:, :half_width], image_values[:, half_width:])
    image_got = swapped(image_sent, "tp", 1)
    image_rows = jnp.concatenate(
        [
            jnp.where(is_second, image_got, image_kept),
            jnp.where(is_second, image_kept, image_got),
        ]
    )

    region_start = jnp.sum(order_int * meta_in[:, 1:2], axis=0)
    region_count = jnp.sum(order_int * meta_in[:, 2:3], axis=0)
    row_ids = column_index * tok_rows + jnp.arange(tok_rows, dtype=jnp.int32)
    row_region = ((row_ids // most_slots)[:, None] == section_ids[None, :]).astype(jnp.int32)
    row_local = row_ids % most_slots
    row_start = jnp.sum(row_region * region_start[None, :], axis=1)
    row_count = jnp.sum(row_region * region_count[None, :], axis=1)
    covered = (row_local >= row_start) & (row_local < row_start + row_count)
    values = jnp.where(covered[:, None], image_rows, text_values)
    return (values, visual_grads)


def solution(mesh):
    placed = (
        P(("section", "fsdp"), None),
        P("section", None, ("fsdp", "tp")),
        P("section"),
        P("section"),
        P(),
        P(("fsdp", "tp"), "section"),
        P(("section", "fsdp"), None),
    )

    return jax.shard_map(
        on_device,
        mesh=mesh,
        in_specs=placed,
        out_specs=(P(("section", "fsdp"), "tp"), P("section", None, ("fsdp", "tp"))),
        check_vma=False,
    )
```
